32 devices in a mesh: sec: 8 (over y, x, core), term: 4 (over z).
Axes of the slice: x: 2, y: 2, z: 4, core: 2. Of those that a mesh axis runs over, the one named last changes fastest.
Arguments:
- meet_env: bfloat16 [8, 24, 256, 256], P('sec', 'term'), may hold values from -0.375 to 0.375
- meet_iso: bfloat16 [8, 256, 2, 256], P('sec'), may hold values from -0.3125 to 0.3125
- last_site: bfloat16 [8, 256, 2, 256], P('sec'), may hold values from -60 to 60
- first_site: bfloat16 [8, 256, 2, 256], P('sec'), may hold values from -0.375 to 0.375
- term_kind: int32 [24, 2], P('term'), may hold values from 0 to 3
Outputs:
- two_site_out: float32 [8, 256, 2, 2, 256], P('sec')
The draws below stay inside these ranges and needn't reach their ends.
All inputs are finite; a program needn't handle non-finite values.
Results may differ from the reference program's by a relative error of at most 0.013.
Values may be sent and summed in bfloat16 or wider, within the bound.
A program may use at most 64 MiB of HBM per device.

```python
import jax
import jax.numpy as jnp
import numpy as np
from jax import lax

BOND = 256
PHYS = 2
TERMS = 24
STEPS = 2
SECS = 8
N_TERM = 4


def draw_last_site(key, part):
    base_key, row_key = jax.random.split(key, 2)
    full_shape = (SECS, BOND, PHYS, BOND)
    base_draw = jax.random.truncated_normal(base_key, -6.0, 6.0, full_shape, jnp.float32)
    row_scale = 10.0 ** jax.random.uniform(row_key, (SECS, BOND, 1, 1), jnp.float32, 0.0, 1.0)
    return (base_draw * row_scale).astype(jnp.bfloat16)


def touch_ends(values, stream_key, smallest, top_value):
    shape = values.shape
    index_at = [jax.random.randint(jax.random.fold_in(stream_key, axis), (), 0, shape[axis]) for axis in range(len(shape))]
    values = values.at[tuple(index_at)].set(smallest)
    longest = shape.index(max(shape))
    index_at[longest] = (index_at[longest] + 1) % shape[longest]
    return values.at[tuple(index_at)].set(top_value)


def shard_levels(rng, extent, shards, low, largest):
    factor_of, own = 1.0, jax.random.fold_in(rng, 6)
    for axis_at, parts in shards:
        heights = jnp.exp(jax.random.uniform(jax.random.fold_in(own, axis_at), (parts,), jnp.float32, low / len(shards), largest / len(shards)))
        factor_of = factor_of * jnp.repeat(heights, extent[axis_at] // parts).reshape([-1 if axis == axis_at else 1 for axis in range(len(extent))])
    return factor_of


def bell_draw(rng, extent, scale, reach, shards=(), kind=jnp.bfloat16):
    drawn = jax.random.normal(rng, extent, jnp.float32) * scale
    if len(shards) > 0:
        drawn = shard_levels(rng, extent, shards, -0.22, 0.18) * drawn
    return jnp.clip(drawn, min=-reach, max=reach).astype(kind)


def setup_inputs(seed: int = 0) -> dict:
    key_list = jax.random.split(jax.random.key(seed), 6)
    meet_env = bell_draw(key_list[0], (SECS, TERMS, BOND, BOND), BOND ** -0.5, 0.375, ((0, 8), (1, 4)))
    meet_iso = bell_draw(key_list[1], (SECS, BOND, PHYS, BOND), (3 * BOND // 2) ** -0.5, 0.3125, ((0, 8),))
    last_site = draw_last_site(jax.random.fold_in(key_list[5], 71), 0)
    first_site = bell_draw(key_list[3], (SECS, BOND, PHYS, BOND), BOND ** -0.5, 0.375, ((0, 8),))
    term_kind = touch_ends(jax.random.randint(key_list[4], (TERMS, 2), 0, 4), jax.random.fold_in(key_list[4], 1), 0, 3).astype(jnp.int32)
    return dict(meet_env=meet_env, meet_iso=meet_iso, last_site=last_site, first_site=first_site, term_kind=term_kind)


operator_table = np.array([[[1.0, 0.0], [0.0, 1.0]], [[0.0, 1.0], [1.0, 0.0]], [[1.0, 0.0], [0.0, -1.0]], [[0.0, 1.0], [-1.0, 0.0]]], dtype=np.float32)
step_size = 0.2
epsilon = 1e-06

def operator_pairs(term_kind):
    levels = jnp.arange(4, dtype=jnp.int32)
    onehot = (term_kind[:, :, None] == levels).astype(jnp.float32)
    return jnp.einsum('kjo,oxy->kjxy', onehot, jnp.asarray(operator_table, dtype=jnp.float32))

def extend(environment, basis, operators):
    wide = jnp.einsum('kab,bsm->kasm', environment.astype(jnp.float32), basis.astype(jnp.float32)).astype(jnp.bfloat16)
    mixed = jnp.einsum('kst,katm->kasm', operators.astype(jnp.float32), wide.astype(jnp.float32)).astype(jnp.bfloat16)
    return jnp.einsum('asm,kasn->kmn', basis.astype(jnp.float32), mixed.astype(jnp.float32)).astype(jnp.bfloat16)

def extend_twice(environment, first_basis, second_basis, operators):
    return extend(extend(environment, first_basis, operators), second_basis, operators)

def apply_terms(vector, left_env, right_env, operators):
    pair_ops = jnp.einsum('ksx,kty->kstxy', operators[:, 0], operators[:, 1]).reshape(operators.shape[0], 4, 4)
    permuted = jnp.einsum('kxy,ayc->kaxc', pair_ops, vector.astype(jnp.float32)).astype(jnp.bfloat16)
    left_applied = jnp.einsum('kab,kbxc->kaxc', left_env.astype(jnp.float32), permuted.astype(jnp.float32)).astype(jnp.bfloat16)
    groups = N_TERM
    per_group = TERMS // N_TERM
    bond_dim = vector.shape[0]
    grouped = jnp.einsum('gkaxc,gkdc->gaxd', left_applied.astype(jnp.float32).reshape(groups, per_group, bond_dim, 4, bond_dim), right_env.astype(jnp.float32).reshape(groups, per_group, bond_dim, bond_dim))
    rounded = lax.optimization_barrier(grouped.astype(jnp.bfloat16))
    return lax.optimization_barrier(jnp.sum(rounded.astype(jnp.float32), axis=0))

def reference(meet_env, meet_iso, last_site, first_site, term_kind):
    operators = operator_pairs(term_kind)
    sections = meet_env.shape[0]
    bond_dim = meet_env.shape[2]

    def fresh_for(section):
        odd_section = section % 2 == 1
        partner = jnp.bitwise_xor(section, 1).astype(jnp.int32)
        partner_iso = meet_iso[partner]
        own_iso = meet_iso[section]
        first_basis = jnp.where(odd_section, partner_iso, jnp.transpose(partner_iso, (2, 1, 0)))
        second_basis = jnp.where(odd_section, own_iso, jnp.transpose(own_iso, (2, 1, 0)))
        chain_ops = jnp.where(odd_section, operators[:, 0], operators[:, 1])
        return extend_twice(meet_env[partner], first_basis, second_basis, chain_ops)
    fresh_env = lax.map(fresh_for, jnp.arange(sections, dtype=jnp.int32))

    def solve_for(section):
        odd_section = section % 2 == 1
        before = ((section + sections - 1) % sections).astype(jnp.int32)
        left_env = jnp.where(odd_section, meet_env[before], fresh_env[before])
        right_env = jnp.where(odd_section, meet_env[section], fresh_env[section])
        two_site = jnp.dot(last_site[before].reshape(2 * bond_dim, bond_dim), first_site[section].reshape(bond_dim, 2 * bond_dim), preferred_element_type=jnp.float32).reshape(bond_dim, 4, bond_dim)
        for step_index in range(STEPS):
            update = apply_terms(two_site.astype(jnp.bfloat16), left_env, right_env, operators)
            two_site = two_site - step_size * update
        norm_scale = lax.rsqrt(jnp.mean(two_site * two_site) + epsilon)
        return (two_site * norm_scale).reshape(bond_dim, PHYS, PHYS, bond_dim)
    return lax.map(solve_for, jnp.arange(sections, dtype=jnp.int32))
```

```python
import functools

import jax
import jax.numpy as jnp
from jax import lax
from jax.experimental import pallas as pl
from jax.experimental.pallas import tpu as pltpu
from jax.sharding import PartitionSpec as P

PHYS = 2
STEPS = 2
step_size = 0.2
epsilon = 1e-06
F32 = jnp.float32
BF16 = jnp.bfloat16
MESH = pl.DeviceIdType.MESH


def matmul(lhs, rhs):
    return jnp.dot(lhs, rhs, preferred_element_type=F32)


def kernel(
    n_sec,
    n_term,
    terms,
    kind_ref,
    env_ref,
    iso_ref,
    last_ref,
    first_ref,
    out_ref,
    envbuf,
    rbuf,
    fresh,
    piso,
    came,
    basis,
    table,
    g,
    v,
    two_site,
    acc,
    tot,
    recv,
    one_send,
    one_recv,
    env_send,
    env_recv,
    fresh_send,
    fresh_recv,
    in_send,
    chunk_recv,
    out_send,
):
    pairs = PHYS * PHYS
    sec = lax.axis_index("sec")
    term = lax.axis_index("term")
    odd = lax.rem(sec, 2)
    is_odd = odd == 1
    is_even = odd == 0
    partner = sec + 1 - 2 * odd
    following = lax.rem(sec + 1, n_sec)
    before = lax.rem(sec + n_sec - 1, n_sec)
    half = n_term // 2
    left_side = term < half
    inward = jnp.where(left_side, term + 1, term - 1)
    outward = jnp.where(left_side, term - 1, term + 1)
    has_outward = jnp.logical_and(term > 0, term < n_term - 1)
    middle = jnp.logical_or(term == half - 1, term == half)
    in_slot = jnp.where(middle, 1, 0)

    def at(s, t):
        return dict(device_id=(s, t), device_id_type=MESH)

    barrier = pltpu.get_barrier_semaphore()
    for s in (following, before):
        pl.semaphore_signal(barrier, inc=1, **at(s, term))
    pl.semaphore_signal(barrier, inc=1, **at(sec, inward))

    @pl.when(has_outward)
    def _():
        pl.semaphore_signal(barrier, inc=1, **at(sec, outward))
        pl.semaphore_wait(barrier, 4)

    @pl.when(jnp.logical_not(has_outward))
    def _():
        pl.semaphore_wait(barrier, 3)

    def remote(src, dst, send, receive, s, t):
        return pltpu.make_async_remote_copy(
            src_ref=src, dst_ref=dst, send_sem=send, recv_sem=receive, **at(s, t)
        )

    iso_copy = remote(iso_ref, piso, one_send.at[0], one_recv.at[0], partner, term)
    last_copy = remote(last_ref, came, one_send.at[1], one_recv.at[1], following, term)

    def env_copy(k):
        return remote(
            env_ref.at[k], envbuf.at[odd, k], env_send.at[k], env_recv.at[k], partner, term
        )

    def fresh_copy(k):
        return remote(
            fresh.at[k], envbuf.at[0, k], fresh_send.at[k], fresh_recv.at[k], following, term
        )

    def in_copy(n, x):
        return remote(
            acc.at[n, x],
            recv.at[n, in_slot, x],
            in_send.at[n, x],
            chunk_recv.at[n, in_slot, x],
            sec,
            inward,
        )

    def out_copy(n, x):
        return remote(
            tot.at[n, x],
            recv.at[n, 1, x],
            out_send.at[n, x],
            chunk_recv.at[n, 1, x],
            sec,
            outward,
        )

    def arrived(n, slot, x):
        return remote(
            acc.at[n, x],
            recv.at[n, slot, x],
            in_send.at[n, x],
            chunk_recv.at[n, slot, x],
            sec,
            inward,
        )

    iso_copy.start()
    for k in range(terms):
        env_copy(k).start()
    last_copy.start()

    def set_basis(which, source):
        @pl.when(is_odd)
        def _():
            for s in range(PHYS):
                value = source[s]
                turned = value.T
                basis[which, s] = value
                table[which, s] = turned
                if s == 1:
                    table[which, 2] = -turned

        @pl.when(is_even)
        def _():
            for s in range(PHYS):
                value = source[s]
                basis[which, s] = value.T
                table[which, s] = value
                if s == 1:
                    table[which, 2] = -value

    set_basis(1, iso_ref)

    @pl.when(is_odd)
    def _():
        def turn(k, carry):
            rbuf[k] = env_ref[k].T
            return carry

        lax.fori_loop(0, terms, turn, 0)

    iso_copy.wait_recv()
    set_basis(0, piso)

    def extend(value, which, kind):
        first = jnp.where(kind == 1, 1, jnp.where(kind == 3, 2, 0))
        second = jnp.where(kind == 0, 1, jnp.where(kind == 2, 2, 0))
        wide_0 = matmul(value, basis[which, 0]).astype(BF16)
        wide_1 = matmul(value, basis[which, 1]).astype(BF16)
        result = matmul(table[which, first], wide_0) + matmul(table[which, second], wide_1)
        return result.astype(BF16)

    def extend_term(k, carry):
        env_copy(k).wait_recv()
        kind = kind_ref[k, 1 - odd]
        value = extend(extend(envbuf[1 - odd, k], 0, kind), 1, kind)

        @pl.when(is_odd)
        def _():
            fresh[k] = value
            fresh_copy(k).start()

        @pl.when(is_even)
        def _():
            rbuf[k] = value.T

        return carry

    lax.fori_loop(0, terms, extend_term, 0)

    last_copy.wait_recv()
    for s in range(PHYS):
        for t in range(PHYS):
            value = matmul(came[s], first_ref[t])
            two_site[PHYS * s + t] = value
            v[PHYS * s + t] = value.astype(BF16)

    def left_term(k, carry):
        @pl.when(is_even)
        def _():
            fresh_copy(k).wait_recv()

        value = envbuf[0, k]
        for x in range(pairs):
            g[k, x] = matmul(value, v[x]).astype(BF16)
        return carry

    lax.fori_loop(0, terms, left_term, 0)

    for n in range(STEPS):

        def right_pair(x, carry):
            s = x // PHYS
            t = lax.rem(x, PHYS)
            total = None
            for k in range(terms):
                kind_0, kind_1 = kind_ref[k, 0], kind_ref[k, 1]
                flip_0, minus_0 = lax.rem(kind_0, 2), kind_0 // 2
                flip_1, minus_1 = lax.rem(kind_1, 2), kind_1 // 2
                from_s = s + flip_0 - 2 * s * flip_0
                from_t = t + flip_1 - 2 * t * flip_1
                sign = (1 - 2 * s * minus_0) * (1 - 2 * t * minus_1)
                value = g[k, PHYS * from_s + from_t] * sign.astype(F32).astype(BF16)
                product = matmul(value, rbuf[k])
                total = product if total is None else total + product
            partial = total.astype(BF16)

            @pl.when(has_outward)
            def _():
                arrived(n, 0, x).wait_recv()
                acc[n, x] = (partial.astype(F32) + recv[n, 0, x].astype(F32)).astype(BF16)

            @pl.when(jnp.logical_not(has_outward))
            def _():
                acc[n, x] = partial

            in_copy(n, x).start()
            return carry

        lax.fori_loop(0, pairs, right_pair, 0)

        def finish_pair(x, squares):
            arrived(n, 1, x).wait_recv()
            came_in = recv[n, 1, x].astype(F32)
            own = jnp.where(middle, 1.0, 0.0)
            whole = (came_in + own * acc[n, x].astype(F32)).astype(BF16)

            @pl.when(has_outward)
            def _():
                tot[n, x] = whole
                out_copy(n, x).start()

            value = two_site[x] - step_size * whole.astype(F32)
            two_site[x] = value
            if n < STEPS - 1:
                rounded = value.astype(BF16)
                for k in range(terms):
                    g[k, x] = matmul(envbuf[0, k], rounded).astype(BF16)
                return squares
            return squares + jnp.sum(value * value)

        squares = lax.fori_loop(0, pairs, finish_pair, jnp.zeros((), F32))

    size = two_site.shape[0] * two_site.shape[1] * two_site.shape[2]
    scale = lax.rsqrt(jnp.full((1, 1), squares, F32) / size + epsilon)

    def write_pair(x, carry):
        out_ref[x] = two_site[x] * scale
        return carry

    lax.fori_loop(0, pairs, write_pair, 0)

    iso_copy.wait_send()
    last_copy.wait_send()

    def drain_term(k, carry):
        env_copy(k).wait_send()

        @pl.when(is_odd)
        def _():
            fresh_copy(k).wait_send()

        return carry

    lax.fori_loop(0, terms, drain_term, 0)
    for n in range(STEPS):

        def drain_pair(x, carry):
            in_copy(n, x).wait_send()

            @pl.when(has_outward)
            def _():
                out_copy(n, x).wait_send()

            return carry

        lax.fori_loop(0, pairs, drain_pair, 0)


def shards(n_sec, n_term, meet_env, meet_iso, last_site, first_site, term_kind):
    terms, bond = meet_env.shape[1], meet_env.shape[2]
    pairs = PHYS * PHYS

    def by_level(site):
        return jnp.transpose(site[0], (1, 0, 2))

    vmem = pl.BlockSpec(memory_space=pltpu.VMEM)
    block = (bond, bond)
    dma = pltpu.SemaphoreType.DMA
    out = pl.pallas_call(
        functools.partial(kernel, n_sec, n_term, terms),
        out_shape=jax.ShapeDtypeStruct((pairs, bond, bond), F32),
        in_specs=[pl.BlockSpec(memory_space=pltpu.SMEM)] + [vmem] * 4,
        out_specs=vmem,
        scratch_shapes=[
            pltpu.VMEM((2, terms) + block, BF16),
            pltpu.VMEM((terms,) + block, BF16),
            pltpu.VMEM((terms,) + block, BF16),
            pltpu.VMEM((PHYS,) + block, BF16),
            pltpu.VMEM((PHYS,) + block, BF16),
            pltpu.VMEM((2, PHYS) + block, BF16),
            pltpu.VMEM((2, 3) + block, BF16),
            pltpu.VMEM((terms, pairs) + block, BF16),
            pltpu.VMEM((pairs,) + block, BF16),
            pltpu.VMEM((pairs,) + block, F32),
            pltpu.VMEM((STEPS, pairs) + block, BF16),
            pltpu.VMEM((STEPS, pairs) + block, BF16),
            pltpu.VMEM((STEPS, 2, pairs) + block, BF16),
            dma((2,)),
            dma((2,)),
            dma((terms,)),
            dma((terms,)),
            dma((terms,)),
            dma((terms,)),
            dma((STEPS, pairs)),
            dma((STEPS, 2, pairs)),
            dma((STEPS, pairs)),
        ],
        compiler_params=pltpu.CompilerParams(
            collective_id=0, has_side_effects=True, vmem_limit_bytes=48 * 1024 * 1024
        ),
    )(term_kind, meet_env[0], by_level(meet_iso), by_level(last_site), by_level(first_site))
    out = jnp.transpose(out, (1, 0, 2))
    return out.reshape(1, bond, PHYS, PHYS, bond)


def solution(mesh):
    in_specs = (
        P("sec", "term", None, None),
        P("sec", None, None, None),
        P("sec", None, None, None),
        P("sec", None, None, None),
        P("term", None),
    )
    out_specs = P("sec", None, None, None, None)
    body = functools.partial(shards, mesh.shape["sec"], mesh.shape["term"])
    return jax.shard_map(body, mesh=mesh, in_specs=in_specs, out_specs=out_specs, check_vma=False)
```

```python
import functools

import jax
import jax.numpy as jnp
from jax import lax
from jax.experimental import pallas as pl
from jax.experimental.pallas import tpu as pltpu
from jax.sharding import PartitionSpec as P

PHYS = 2
STEPS = 2
PARTS = 4
LAG = 5
step_size = 0.2
epsilon = 1e-06
F32 = jnp.float32
BF16 = jnp.bfloat16
MESH = pl.DeviceIdType.MESH


def matmul(lhs, rhs):
    return jnp.dot(lhs, rhs, preferred_element_type=F32)


def kernel(
    n_sec,
    n_term,
    terms,
    kind_ref,
    env_ref,
    iso_ref,
    last_ref,
    first_ref,
    out_ref,
    envbuf,
    rbuf,
    fresh,
    piso,
    came,
    basis,
    table,
    g,
    v,
    two_site,
    acc,
    tot,
    recv,
    one_send,
    one_recv,
    env_send,
    env_recv,
    fresh_send,
    fresh_recv,
    in_send,
    chunk_recv,
    out_send,
):
    pairs = PHYS * PHYS
    sec = lax.axis_index("sec")
    term = lax.axis_index("term")
    odd = lax.rem(sec, 2)
    is_odd = odd == 1
    is_even = odd == 0
    partner = sec + 1 - 2 * odd
    following = lax.rem(sec + 1, n_sec)
    before = lax.rem(sec + n_sec - 1, n_sec)
    half = n_term // 2
    left_side = term < half
    inward = jnp.where(left_side, term + 1, term - 1)
    outward = jnp.where(left_side, term - 1, term + 1)
    has_outward = jnp.logical_and(term > 0, term < n_term - 1)
    middle = jnp.logical_or(term == half - 1, term == half)
    in_slot = jnp.where(middle, 1, 0)

    def at(s, t):
        return dict(device_id=(s, t), device_id_type=MESH)

    barrier = pltpu.get_barrier_semaphore()
    for s in (following, before):
        pl.semaphore_signal(barrier, inc=1, **at(s, term))
    pl.semaphore_signal(barrier, inc=1, **at(sec, inward))

    @pl.when(has_outward)
    def _():
        pl.semaphore_signal(barrier, inc=1, **at(sec, outward))
        pl.semaphore_wait(barrier, 4)

    @pl.when(jnp.logical_not(has_outward))
    def _():
        pl.semaphore_wait(barrier, 3)

    def remote(src, dst, send, receive, s, t):
        return pltpu.make_async_remote_copy(
            src_ref=src, dst_ref=dst, send_sem=send, recv_sem=receive, **at(s, t)
        )

    iso_copy = remote(iso_ref, piso, one_send.at[0], one_recv.at[0], partner, term)
    last_copy = remote(last_ref, came, one_send.at[1], one_recv.at[1], following, term)

    def env_copy(k):
        return remote(
            env_ref.at[k], envbuf.at[odd, k], env_send.at[k], env_recv.at[k], partner, term
        )

    def fresh_copy(k):
        return remote(
            fresh.at[k], envbuf.at[0, k], fresh_send.at[k], fresh_recv.at[k], following, term
        )

    def in_copy(n, x):
        return remote(
            acc.at[n, x],
            recv.at[n, in_slot, x],
            in_send.at[n, x],
            chunk_recv.at[n, in_slot, x],
            sec,
            inward,
        )

    def out_copy(n, x):
        return remote(
            tot.at[n, x],
            recv.at[n, 1, x],
            out_send.at[n, x],
            chunk_recv.at[n, 1, x],
            sec,
            outward,
        )

    def arrived(n, slot, x):
        return remote(
            acc.at[n, x],
            recv.at[n, slot, x],
            in_send.at[n, x],
            chunk_recv.at[n, slot, x],
            sec,
            inward,
        )

    iso_copy.start()
    for k in range(terms):
        env_copy(k).start()
    last_copy.start()

    def set_basis(which, source):
        @pl.when(is_odd)
        def _():
            for s in range(PHYS):
                value = source[s]
                turned = value.T
                basis[which, s] = value
                table[which, s] = turned
                if s == 1:
                    table[which, 2] = -turned

        @pl.when(is_even)
        def _():
            for s in range(PHYS):
                value = source[s]
                basis[which, s] = value.T
                table[which, s] = value
                if s == 1:
                    table[which, 2] = -value

    set_basis(1, iso_ref)

    @pl.when(is_odd)
    def _():
        def turn(k, carry):
            rbuf[k] = env_ref[k].T
            return carry

        lax.fori_loop(0, terms, turn, 0)

    iso_copy.wait_recv()
    set_basis(0, piso)

    def extend(value, which, kind):
        first = jnp.where(kind == 1, 1, jnp.where(kind == 3, 2, 0))
        second = jnp.where(kind == 0, 1, jnp.where(kind == 2, 2, 0))
        wide_0 = matmul(value, basis[which, 0]).astype(BF16)
        wide_1 = matmul(value, basis[which, 1]).astype(BF16)
        result = matmul(table[which, first], wide_0) + matmul(table[which, second], wide_1)
        return result.astype(BF16)

    def extend_term(k, carry):
        env_copy(k).wait_recv()
        kind = kind_ref[k, 1 - odd]
        value = extend(extend(envbuf[1 - odd, k], 0, kind), 1, kind)

        @pl.when(is_odd)
        def _():
            fresh[k] = value
            fresh_copy(k).start()

        @pl.when(is_even)
        def _():
            rbuf[k] = value.T

        return carry

    lax.fori_loop(0, terms, extend_term, 0)

    last_copy.wait_recv()
    for s in range(PHYS):
        for t in range(PHYS):
            value = matmul(came[s], first_ref[t])
            two_site[PHYS * s + t] = value
            v[PHYS * s + t] = value.astype(BF16)

    def left_term(k, carry):
        @pl.when(is_even)
        def _():
            fresh_copy(k).wait_recv()

        value = envbuf[0, k]
        for x in range(pairs):
            g[0, k, x] = matmul(value, v[x]).astype(BF16)
        return carry

    lax.fori_loop(0, terms, left_term, 0)

    rows = two_site.shape[1] // PARTS
    chunks = pairs * PARTS

    def partial_of(n, x):
        s = x // PHYS
        t = lax.rem(x, PHYS)
        total = None
        for k in range(terms):
            kind_0, kind_1 = kind_ref[k, 0], kind_ref[k, 1]
            flip_0, minus_0 = lax.rem(kind_0, 2), kind_0 // 2
            flip_1, minus_1 = lax.rem(kind_1, 2), kind_1 // 2
            from_s = s + flip_0 - 2 * s * flip_0
            from_t = t + flip_1 - 2 * t * flip_1
            sign = (1 - 2 * s * minus_0) * (1 - 2 * t * minus_1)
            value = g[n, k, PHYS * from_s + from_t] * sign.astype(F32).astype(BF16)
            product = matmul(value, rbuf[k])
            total = product if total is None else total + product
        total = total.astype(BF16)
        for part in range(PARTS):
            acc[n, PARTS * x + part] = total[part * rows : (part + 1) * rows]

    def pass_inward(n, j):
        @pl.when(has_outward)
        def _():
            arrived(n, 0, j).wait_recv()
            acc[n, j] = (acc[n, j].astype(F32) + recv[n, 0, j].astype(F32)).astype(BF16)

        in_copy(n, j).start()

    def pass_outward(n, j, squares):
        arrived(n, 1, j).wait_recv()
        came_in = recv[n, 1, j].astype(F32)
        own = jnp.where(middle, 1.0, 0.0)
        whole = (came_in + own * acc[n, j].astype(F32)).astype(BF16)

        @pl.when(has_outward)
        def _():
            tot[n, j] = whole
            out_copy(n, j).start()

        x = j // PARTS
        span = pl.ds(pl.multiple_of(lax.rem(j, PARTS) * rows, rows), rows)
        value = two_site[x, span] - step_size * whole.astype(F32)
        two_site[x, span] = value
        if n < STEPS - 1:
            v[x, span] = value.astype(BF16)
            return squares
        return squares + jnp.sum(value * value)

    def left_of(n, x):
        for k in range(terms):
            g[n, k, x] = matmul(envbuf[0, k], v[x]).astype(BF16)

    zero = jnp.zeros((), F32)
    for n in range(STEPS):

        def step(j, squares):
            @pl.when(jnp.logical_and(j < chunks, lax.rem(j, PARTS) == 0))
            def _():
                partial_of(n, j // PARTS)

            @pl.when(j < chunks)
            def _():
                pass_inward(n, j)

            return squares

        def head(j, squares):
            return step(j, squares)

        def body(j, squares):
            squares = step(j, squares)
            done = j - LAG
            squares = pass_outward(n, done, squares)
            if n < STEPS - 1:

                @pl.when(lax.rem(done, PARTS) == PARTS - 1)
                def _():
                    left_of(n + 1, done // PARTS)

            return squares

        lax.fori_loop(0, LAG, head, 0)
        squares = lax.fori_loop(LAG, chunks + LAG, body, zero)

    size = two_site.shape[0] * two_site.shape[1] * two_site.shape[2]
    scale = lax.rsqrt(jnp.full((1, 1), squares, F32) / size + epsilon)

    def write_pair(x, carry):
        out_ref[x] = two_site[x] * scale
        return carry

    lax.fori_loop(0, pairs, write_pair, 0)

    iso_copy.wait_send()
    last_copy.wait_send()

    def drain_term(k, carry):
        env_copy(k).wait_send()

        @pl.when(is_odd)
        def _():
            fresh_copy(k).wait_send()

        return carry

    lax.fori_loop(0, terms, drain_term, 0)
    for n in range(STEPS):

        def drain_chunk(x, carry):
            in_copy(n, x).wait_send()

            @pl.when(has_outward)
            def _():
                out_copy(n, x).wait_send()

            return carry

        lax.fori_loop(0, chunks, drain_chunk, 0)


def shards(n_sec, n_term, meet_env, meet_iso, last_site, first_site, term_kind):
    terms, bond = meet_env.shape[1], meet_env.shape[2]
    pairs = PHYS * PHYS

    def by_level(site):
        return jnp.transpose(site[0], (1, 0, 2))

    vmem = pl.BlockSpec(memory_space=pltpu.VMEM)
    block = (bond, bond)
    chunks = pairs * PARTS
    strip = (bond // PARTS, bond)
    dma = pltpu.SemaphoreType.DMA
    out = pl.pallas_call(
        functools.partial(kernel, n_sec, n_term, terms),
        out_shape=jax.ShapeDtypeStruct((pairs, bond, bond), F32),
        in_specs=[pl.BlockSpec(memory_space=pltpu.SMEM)] + [vmem] * 4,
        out_specs=vmem,
        scratch_shapes=[
            pltpu.VMEM((2, terms) + block, BF16),
            pltpu.VMEM((terms,) + block, BF16),
            pltpu.VMEM((terms,) + block, BF16),
            pltpu.VMEM((PHYS,) + block, BF16),
            pltpu.VMEM((PHYS,) + block, BF16),
            pltpu.VMEM((2, PHYS) + block, BF16),
            pltpu.VMEM((2, 3) + block, BF16),
            pltpu.VMEM((STEPS, terms, pairs) + block, BF16),
            pltpu.VMEM((pairs,) + block, BF16),
            pltpu.VMEM((pairs,) + block, F32),
            pltpu.VMEM((STEPS, chunks) + strip, BF16),
            pltpu.VMEM((STEPS, chunks) + strip, BF16),
            pltpu.VMEM((STEPS, 2, chunks) + strip, BF16),
            dma((2,)),
            dma((2,)),
            dma((terms,)),
            dma((terms,)),
            dma((terms,)),
            dma((terms,)),
            dma((STEPS, chunks)),
            dma((STEPS, 2, chunks)),
            dma((STEPS, chunks)),
        ],
        compiler_params=pltpu.CompilerParams(
            collective_id=0, has_side_effects=True, vmem_limit_bytes=48 * 1024 * 1024
        ),
    )(term_kind, meet_env[0], by_level(meet_iso), by_level(last_site), by_level(first_site))
    out = jnp.transpose(out, (1, 0, 2))
    return out.reshape(1, bond, PHYS, PHYS, bond)


def solution(mesh):
    in_specs = (
        P("sec", "term", None, None),
        P("sec", None, None, None),
        P("sec", None, None, None),
        P("sec", None, None, None),
        P("term", None),
    )
    out_specs = P("sec", None, None, None, None)
    body = functools.partial(shards, mesh.shape["sec"], mesh.shape["term"])
    return jax.shard_map(body, mesh=mesh, in_specs=in_specs, out_specs=out_specs, check_vma=False)
```

```python
import functools

import jax
import jax.numpy as jnp
from jax import lax
from jax.experimental import pallas as pl
from jax.experimental.pallas import tpu as pltpu
from jax.sharding import PartitionSpec as P

PHYS = 2
STEPS = 2
PARTS = 4
LAG = 6
GROUP = 2
step_size = 0.2
epsilon = 1e-06
F32 = jnp.float32
BF16 = jnp.bfloat16
MESH = pl.DeviceIdType.MESH


def matmul(lhs, rhs):
    return jnp.dot(lhs, rhs, preferred_element_type=F32)


def kernel(
    n_sec,
    n_term,
    terms,
    kind_ref,
    env_ref,
    iso_ref,
    last_ref,
    first_ref,
    out_ref,
    envbuf,
    rbuf,
    fresh,
    piso,
    came,
    basis,
    table,
    h,
    v,
    two_site,
    early,
    acc,
    tot,
    recv,
    one_send,
    one_recv,
    env_send,
    env_recv,
    fresh_send,
    fresh_recv,
    in_send,
    chunk_recv,
    out_send,
):
    pairs = PHYS * PHYS
    sec = lax.axis_index("sec")
    term = lax.axis_index("term")
    odd = lax.rem(sec, 2)
    is_odd = odd == 1
    is_even = odd == 0
    partner = sec + 1 - 2 * odd
    following = lax.rem(sec + 1, n_sec)
    before = lax.rem(sec + n_sec - 1, n_sec)
    half = n_term // 2
    left_side = term < half
    inward = jnp.where(left_side, term + 1, term - 1)
    outward = jnp.where(left_side, term - 1, term + 1)
    has_outward = jnp.logical_and(term > 0, term < n_term - 1)
    middle = jnp.logical_or(term == half - 1, term == half)
    in_slot = jnp.where(middle, 1, 0)

    def at(s, t):
        return dict(device_id=(s, t), device_id_type=MESH)

    barrier = pltpu.get_barrier_semaphore()
    for s in (following, before):
        pl.semaphore_signal(barrier, inc=1, **at(s, term))
    pl.semaphore_signal(barrier, inc=1, **at(sec, inward))

    @pl.when(has_outward)
    def _():
        pl.semaphore_signal(barrier, inc=1, **at(sec, outward))
        pl.semaphore_wait(barrier, 4)

    @pl.when(jnp.logical_not(has_outward))
    def _():
        pl.semaphore_wait(barrier, 3)

    def remote(src, dst, send, receive, s, t):
        return pltpu.make_async_remote_copy(
            src_ref=src, dst_ref=dst, send_sem=send, recv_sem=receive, **at(s, t)
        )

    iso_copy = remote(iso_ref, piso, one_send.at[0], one_recv.at[0], partner, term)
    last_copy = remote(last_ref, came, one_send.at[1], one_recv.at[1], following, term)

    def env_copy(k):
        return remote(
            env_ref.at[k], envbuf.at[odd, k], env_send.at[k], env_recv.at[k], partner, term
        )

    def fresh_copy(k):
        return remote(
            fresh.at[k], envbuf.at[0, k], fresh_send.at[k], fresh_recv.at[k], following, term
        )

    def in_copy(n, x):
        return remote(
            acc.at[n, x],
            recv.at[n, in_slot, x],
            in_send.at[n, x],
            chunk_recv.at[n, in_slot, x],
            sec,
            inward,
        )

    def out_copy(n, x):
        return remote(
            tot.at[n, x],
            recv.at[n, 1, x],
            out_send.at[n, x],
            chunk_recv.at[n, 1, x],
            sec,
            outward,
        )

    def arrived(n, slot, x):
        return remote(
            acc.at[n, x],
            recv.at[n, slot, x],
            in_send.at[n, x],
            chunk_recv.at[n, slot, x],
            sec,
            inward,
        )

    iso_copy.start()
    for k in range(terms):
        env_copy(k).start()
    last_copy.start()

    def set_basis(which, source):
        @pl.when(is_odd)
        def _():
            for s in range(PHYS):
                value = source[s]
                turned = value.T
                basis[which, s] = value
                table[which, s] = turned
                if s == 1:
                    table[which, 2] = -turned

        @pl.when(is_even)
        def _():
            for s in range(PHYS):
                value = source[s]
                basis[which, s] = value.T
                table[which, s] = value
                if s == 1:
                    table[which, 2] = -value

    set_basis(1, iso_ref)

    @pl.when(is_odd)
    def _():
        def turn(k, carry):
            rbuf[k] = env_ref[k].T
            return carry

        lax.fori_loop(0, terms, turn, 0)

    iso_copy.wait_recv()
    set_basis(0, piso)

    def extend(values, which, kinds):
        wide = [
            [matmul(value, basis[which, r]).astype(BF16) for r in range(PHYS)] for value in values
        ]
        results = []
        for (wide_0, wide_1), kind in zip(wide, kinds):
            first = jnp.where(kind == 1, 1, jnp.where(kind == 3, 2, 0))
            second = jnp.where(kind == 0, 1, jnp.where(kind == 2, 2, 0))
            result = matmul(table[which, first], wide_0) + matmul(table[which, second], wide_1)
            results.append(result.astype(BF16))
        return results

    group = GROUP if terms % GROUP == 0 else 1

    def extend_group(i, carry):
        members = [group * i + m for m in range(group)]
        for k in members:
            env_copy(k).wait_recv()
        kinds = [kind_ref[k, 1 - odd] for k in members]
        values = extend([envbuf[1 - odd, k] for k in members], 0, kinds)
        values = extend(values, 1, kinds)

        @pl.when(is_odd)
        def _():
            for k, value in zip(members, values):
                fresh[k] = value
                fresh_copy(k).start()

        @pl.when(is_even)
        def _():
            for k, value in zip(members, values):
                rbuf[k] = value.T

        return carry

    lax.fori_loop(0, terms // group, extend_group, 0)

    last_copy.wait_recv()
    for s in range(PHYS):
        for t in range(PHYS):
            value = matmul(came[s], first_ref[t])
            two_site[PHYS * s + t] = value
            v[PHYS * s + t] = value.astype(BF16)

    def right_of(n, x):
        value = v[x]
        for k in range(terms):
            h[n, k, x] = matmul(value, rbuf[k]).astype(BF16)

    def first_right(x, carry):
        right_of(0, x)
        return carry

    lax.fori_loop(0, pairs, first_right, 0)

    def term_of(n, k, x):
        s = x // PHYS
        t = lax.rem(x, PHYS)
        kind_0, kind_1 = kind_ref[k, 0], kind_ref[k, 1]
        flip_0, minus_0 = lax.rem(kind_0, 2), kind_0 // 2
        flip_1, minus_1 = lax.rem(kind_1, 2), kind_1 // 2
        from_s = s + flip_0 - 2 * s * flip_0
        from_t = t + flip_1 - 2 * t * flip_1
        sign = (1 - 2 * s * minus_0) * (1 - 2 * t * minus_1)
        value = h[n, k, PHYS * from_s + from_t] * sign.astype(F32).astype(BF16)
        return matmul(envbuf[0, k], value)

    @pl.when(is_even)
    def _():
        for x in range(pairs):
            early[x] = jnp.zeros(early.shape[1:], F32)

        def early_term(k, carry):
            fresh_copy(k).wait_recv()
            for x in range(pairs):
                early[x] += term_of(0, k, x)
            return carry

        lax.fori_loop(0, terms - 1, early_term, 0)
        fresh_copy(terms - 1).wait_recv()

    rows = two_site.shape[1] // PARTS
    chunks = pairs * PARTS

    def put_partial(n, x, total):
        total = total.astype(BF16)
        for part in range(PARTS):
            acc[n, PARTS * x + part] = total[part * rows : (part + 1) * rows]

    def full_partial(n, x):
        total = term_of(n, 0, x)
        for k in range(1, terms):
            total = total + term_of(n, k, x)
        put_partial(n, x, total)

    def partial_of(n, x):
        if n > 0:
            full_partial(n, x)
            return

        @pl.when(is_odd)
        def _():
            full_partial(n, x)

        @pl.when(is_even)
        def _():
            put_partial(n, x, early[x] + term_of(n, terms - 1, x))

    def pass_inward(n, j):
        @pl.when(has_outward)
        def _():
            arrived(n, 0, j).wait_recv()
            acc[n, j] = (acc[n, j].astype(F32) + recv[n, 0, j].astype(F32)).astype(BF16)

        in_copy(n, j).start()

    def pass_outward(n, j, squares):
        arrived(n, 1, j).wait_recv()
        came_in = recv[n, 1, j].astype(F32)
        own = jnp.where(middle, 1.0, 0.0)
        whole = (came_in + own * acc[n, j].astype(F32)).astype(BF16)

        @pl.when(has_outward)
        def _():
            tot[n, j] = whole
            out_copy(n, j).start()

        x = j // PARTS
        span = pl.ds(pl.multiple_of(lax.rem(j, PARTS) * rows, rows), rows)
        value = two_site[x, span] - step_size * whole.astype(F32)
        two_site[x, span] = value
        if n < STEPS - 1:
            v[x, span] = value.astype(BF16)
            return squares
        return squares + jnp.sum(value * value)

    lag = jnp.where(has_outward, min(LAG, chunks), chunks)
    zero = jnp.zeros((), F32)
    for n in range(STEPS):

        def step(j, squares):
            @pl.when(jnp.logical_and(j < chunks, lax.rem(j, PARTS) == 0))
            def _():
                partial_of(n, j // PARTS)

            @pl.when(j < chunks)
            def _():
                pass_inward(n, j)

            return squares

        def head(j, squares):
            return step(j, squares)

        def body(j, squares):
            squares = step(j, squares)
            done = j - lag
            squares = pass_outward(n, done, squares)
            if n < STEPS - 1:

                @pl.when(lax.rem(done, PARTS) == PARTS - 1)
                def _():
                    right_of(n + 1, done // PARTS)

            return squares

        lax.fori_loop(0, lag, head, 0)
        squares = lax.fori_loop(lag, chunks + lag, body, zero)

    size = two_site.shape[0] * two_site.shape[1] * two_site.shape[2]
    scale = lax.rsqrt(jnp.full((1, 1), squares, F32) / size + epsilon)

    lanes = out_ref.shape[1]
    halves = two_site.shape[2] // lanes
    stride = PHYS * PHYS * halves
    for s in range(PHYS):
        for t in range(PHYS):
            for c in range(halves):
                span = pl.ds((s * halves + c) * PHYS + t, two_site.shape[1], stride=stride)
                columns = pl.ds(c * lanes, lanes)
                out_ref[span, :] = two_site[PHYS * s + t, :, columns] * scale

    iso_copy.wait_send()
    last_copy.wait_send()

    def drain_term(k, carry):
        env_copy(k).wait_send()

        @pl.when(is_odd)
        def _():
            fresh_copy(k).wait_send()

        return carry

    lax.fori_loop(0, terms, drain_term, 0)
    for n in range(STEPS):

        def drain_chunk(x, carry):
            in_copy(n, x).wait_send()

            @pl.when(has_outward)
            def _():
                out_copy(n, x).wait_send()

            return carry

        lax.fori_loop(0, chunks, drain_chunk, 0)


def shards(n_sec, n_term, meet_env, meet_iso, last_site, first_site, term_kind):
    terms, bond = meet_env.shape[1], meet_env.shape[2]
    pairs = PHYS * PHYS

    def by_level(site):
        return jnp.transpose(site[0], (1, 0, 2))

    vmem = pl.BlockSpec(memory_space=pltpu.VMEM)
    block = (bond, bond)
    chunks = pairs * PARTS
    strip = (bond // PARTS, bond)
    lanes = min(bond, 128)
    dma = pltpu.SemaphoreType.DMA
    out = pl.pallas_call(
        functools.partial(kernel, n_sec, n_term, terms),
        out_shape=jax.ShapeDtypeStruct((pairs * bond * bond // lanes, lanes), F32),
        in_specs=[pl.BlockSpec(memory_space=pltpu.SMEM)] + [vmem] * 4,
        out_specs=vmem,
        scratch_shapes=[
            pltpu.VMEM((2, terms) + block, BF16),
            pltpu.VMEM((terms,) + block, BF16),
            pltpu.VMEM((terms,) + block, BF16),
            pltpu.VMEM((PHYS,) + block, BF16),
            pltpu.VMEM((PHYS,) + block, BF16),
            pltpu.VMEM((2, PHYS) + block, BF16),
            pltpu.VMEM((2, 3) + block, BF16),
            pltpu.VMEM((STEPS, terms, pairs) + block, BF16),
            pltpu.VMEM((pairs,) + block, BF16),
            pltpu.VMEM((pairs,) + block, F32),
            pltpu.VMEM((pairs,) + block, F32),
            pltpu.VMEM((STEPS, chunks) + strip, BF16),
            pltpu.VMEM((STEPS, chunks) + strip, BF16),
            pltpu.VMEM((STEPS, 2, chunks) + strip, BF16),
            dma((2,)),
            dma((2,)),
            dma((terms,)),
            dma((terms,)),
            dma((terms,)),
            dma((terms,)),
            dma((STEPS, chunks)),
            dma((STEPS, 2, chunks)),
            dma((STEPS, chunks)),
        ],
        compiler_params=pltpu.CompilerParams(
            collective_id=0, has_side_effects=True, vmem_limit_bytes=48 * 1024 * 1024
        ),
    )(term_kind, meet_env[0], by_level(meet_iso), by_level(last_site), by_level(first_site))
    out = out.reshape(bond, PHYS, bond // lanes, PHYS, lanes)
    out = jnp.transpose(out, (0, 1, 3, 2, 4))
    return out.reshape(1, bond, PHYS, PHYS, bond)


def solution(mesh):
    in_specs = (
        P("sec", "term", None, None),
        P("sec", None, None, None),
        P("sec", None, None, None),
        P("sec", None, None, None),
        P("term", None),
    )
    out_specs = P("sec", None, None, None, None)
    body = functools.partial(shards, mesh.shape["sec"], mesh.shape["term"])
    return jax.shard_map(body, mesh=mesh, in_specs=in_specs, out_specs=out_specs, check_vma=False)
```

```python
import functools

import jax
import jax.numpy as jnp
from jax import lax
from jax.experimental import pallas as pl
from jax.experimental.pallas import tpu as pltpu
from jax.sharding import PartitionSpec as P

PHYS = 2
STEPS = 2
PARTS = 4
LAG = 9
GROUP = 2
step_size = 0.2
epsilon = 1e-06
F32 = jnp.float32
BF16 = jnp.bfloat16
MESH = pl.DeviceIdType.MESH


def matmul(lhs, rhs):
    return jnp.dot(lhs, rhs, preferred_element_type=F32)


def kernel(
    n_sec,
    n_term,
    terms,
    kind_ref,
    env_ref,
    iso_ref,
    last_ref,
    first_ref,
    out_ref,
    envbuf,
    rbuf,
    fresh,
    piso,
    came,
    basis,
    table,
    h,
    v,
    two_site,
    early,
    acc,
    tot,
    recv,
    one_send,
    one_recv,
    env_send,
    env_recv,
    fresh_send,
    fresh_recv,
    in_send,
    chunk_recv,
    out_send,
):
    pairs = PHYS * PHYS
    sec = lax.axis_index("sec")
    term = lax.axis_index("term")
    odd = lax.rem(sec, 2)
    is_odd = odd == 1
    is_even = odd == 0
    partner = sec + 1 - 2 * odd
    following = lax.rem(sec + 1, n_sec)
    before = lax.rem(sec + n_sec - 1, n_sec)
    half = n_term // 2
    left_side = term < half
    inward = jnp.where(left_side, term + 1, term - 1)
    outward = jnp.where(left_side, term - 1, term + 1)
    has_outward = jnp.logical_and(term > 0, term < n_term - 1)
    middle = jnp.logical_or(term == half - 1, term == half)
    in_slot = jnp.where(middle, 1, 0)

    def at(s, t):
        return dict(device_id=(s, t), device_id_type=MESH)

    barrier = pltpu.get_barrier_semaphore()
    for s in (following, before):
        pl.semaphore_signal(barrier, inc=1, **at(s, term))
    pl.semaphore_signal(barrier, inc=1, **at(sec, inward))

    @pl.when(has_outward)
    def _():
        pl.semaphore_signal(barrier, inc=1, **at(sec, outward))
        pl.semaphore_wait(barrier, 4)

    @pl.when(jnp.logical_not(has_outward))
    def _():
        pl.semaphore_wait(barrier, 3)

    def remote(src, dst, send, receive, s, t):
        return pltpu.make_async_remote_copy(
            src_ref=src, dst_ref=dst, send_sem=send, recv_sem=receive, **at(s, t)
        )

    iso_copy = remote(iso_ref, piso, one_send.at[0], one_recv.at[0], partner, term)
    last_copy = remote(last_ref, came, one_send.at[1], one_recv.at[1], following, term)

    def env_copy(k):
        return remote(
            env_ref.at[k], envbuf.at[odd, k], env_send.at[k], env_recv.at[k], partner, term
        )

    def fresh_copy(k):
        return remote(
            fresh.at[k], envbuf.at[0, k], fresh_send.at[k], fresh_recv.at[k], following, term
        )

    def in_copy(n, x):
        return remote(
            acc.at[n, x],
            recv.at[n, in_slot, x],
            in_send.at[n, x],
            chunk_recv.at[n, in_slot, x],
            sec,
            inward,
        )

    def out_copy(n, x):
        return remote(
            tot.at[n, x],
            recv.at[n, 1, x],
            out_send.at[n, x],
            chunk_recv.at[n, 1, x],
            sec,
            outward,
        )

    def arrived(n, slot, x):
        return remote(
            acc.at[n, x],
            recv.at[n, slot, x],
            in_send.at[n, x],
            chunk_recv.at[n, slot, x],
            sec,
            inward,
        )

    iso_copy.start()
    for k in range(terms):
        env_copy(k).start()
    last_copy.start()

    def set_basis(which, source):
        @pl.when(is_odd)
        def _():
            for s in range(PHYS):
                value = source[s]
                turned = value.T
                basis[which, s] = value
                table[which, s] = turned
                if s == 1:
                    table[which, 2] = -turned

        @pl.when(is_even)
        def _():
            for s in range(PHYS):
                value = source[s]
                basis[which, s] = value.T
                table[which, s] = value
                if s == 1:
                    table[which, 2] = -value

    set_basis(1, iso_ref)

    @pl.when(is_odd)
    def _():
        def turn(k, carry):
            rbuf[k] = env_ref[k].T
            return carry

        lax.fori_loop(0, terms, turn, 0)

    iso_copy.wait_recv()
    set_basis(0, piso)

    def extend(values, which, kinds):
        wide = [
            [matmul(value, basis[which, r]).astype(BF16) for r in range(PHYS)] for value in values
        ]
        results = []
        for (wide_0, wide_1), kind in zip(wide, kinds):
            first = jnp.where(kind == 1, 1, jnp.where(kind == 3, 2, 0))
            second = jnp.where(kind == 0, 1, jnp.where(kind == 2, 2, 0))
            result = matmul(table[which, first], wide_0) + matmul(table[which, second], wide_1)
            results.append(result.astype(BF16))
        return results

    group = GROUP if terms % GROUP == 0 else 1

    def extend_group(i, carry):
        members = [group * i + m for m in range(group)]
        for k in members:
            env_copy(k).wait_recv()
        kinds = [kind_ref[k, 1 - odd] for k in members]
        values = extend([envbuf[1 - odd, k] for k in members], 0, kinds)
        values = extend(values, 1, kinds)

        @pl.when(is_odd)
        def _():
            for k, value in zip(members, values):
                fresh[k] = value
                fresh_copy(k).start()

        @pl.when(is_even)
        def _():
            for k, value in zip(members, values):
                rbuf[k] = value.T

        return carry

    lax.fori_loop(0, terms // group, extend_group, 0)

    last_copy.wait_recv()
    for s in range(PHYS):
        for t in range(PHYS):
            value = matmul(came[s], first_ref[t])
            two_site[PHYS * s + t] = value
            v[PHYS * s + t] = value.astype(BF16)

    def right_of(n, x):
        value = v[x]
        for k in range(terms):
            h[n, k, x] = matmul(value, rbuf[k]).astype(BF16)

    def first_right(x, carry):
        right_of(0, x)
        return carry

    lax.fori_loop(0, pairs, first_right, 0)

    def term_of(n, k, x):
        s = x // PHYS
        t = lax.rem(x, PHYS)
        kind_0, kind_1 = kind_ref[k, 0], kind_ref[k, 1]
        flip_0, minus_0 = lax.rem(kind_0, 2), kind_0 // 2
        flip_1, minus_1 = lax.rem(kind_1, 2), kind_1 // 2
        from_s = s + flip_0 - 2 * s * flip_0
        from_t = t + flip_1 - 2 * t * flip_1
        sign = (1 - 2 * s * minus_0) * (1 - 2 * t * minus_1)
        value = h[n, k, PHYS * from_s + from_t] * sign.astype(F32).astype(BF16)
        return matmul(envbuf[0, k], value)

    @pl.when(is_even)
    def _():
        for x in range(pairs):
            early[x] = jnp.zeros(early.shape[1:], F32)

        def early_term(k, carry):
            fresh_copy(k).wait_recv()
            for x in range(pairs):
                early[x] += term_of(0, k, x)
            return carry

        lax.fori_loop(0, terms - 1, early_term, 0)
        fresh_copy(terms - 1).wait_recv()

    rows = two_site.shape[1] // PARTS
    chunks = pairs * PARTS

    def put_partial(n, x, total):
        total = total.astype(BF16)
        for part in range(PARTS):
            acc[n, PARTS * x + part] = total[part * rows : (part + 1) * rows]

    def full_partial(n, x):
        total = term_of(n, 0, x)
        for k in range(1, terms):
            total = total + term_of(n, k, x)
        put_partial(n, x, total)

    def partial_of(n, x):
        if n > 0:
            full_partial(n, x)
            return

        @pl.when(is_odd)
        def _():
            full_partial(n, x)

        @pl.when(is_even)
        def _():
            put_partial(n, x, early[x] + term_of(n, terms - 1, x))

    def pass_inward(n, j):
        @pl.when(has_outward)
        def _():
            arrived(n, 0, j).wait_recv()
            acc[n, j] = (acc[n, j].astype(F32) + recv[n, 0, j].astype(F32)).astype(BF16)

        in_copy(n, j).start()

    def pass_outward(n, j, squares):
        arrived(n, 1, j).wait_recv()
        came_in = recv[n, 1, j].astype(F32)
        own = jnp.where(middle, 1.0, 0.0)
        whole = (came_in + own * acc[n, j].astype(F32)).astype(BF16)

        @pl.when(has_outward)
        def _():
            tot[n, j] = whole
            out_copy(n, j).start()

        x = j // PARTS
        span = pl.ds(pl.multiple_of(lax.rem(j, PARTS) * rows, rows), rows)
        value = two_site[x, span] - step_size * whole.astype(F32)
        two_site[x, span] = value
        if n < STEPS - 1:
            v[x, span] = value.astype(BF16)
            return squares
        return squares + jnp.sum((value * value).reshape((rows // 8, 8, value.shape[1])), axis=0)

    lag = jnp.where(has_outward, min(LAG, chunks), chunks)
    zero = jnp.zeros((8, two_site.shape[2]), F32)
    for n in range(STEPS):

        def step(j, squares):
            @pl.when(jnp.logical_and(j < chunks, lax.rem(j, PARTS) == 0))
            def _():
                partial_of(n, j // PARTS)

            @pl.when(j < chunks)
            def _():
                pass_inward(n, j)

            return squares

        def head(j, squares):
            return step(j, squares)

        def body(j, squares):
            squares = step(j, squares)
            done = j - lag
            squares = pass_outward(n, done, squares)
            if n < STEPS - 1:

                @pl.when(lax.rem(done, PARTS) == PARTS - 1)
                def _():
                    right_of(n + 1, done // PARTS)

            return squares

        lax.fori_loop(0, lag, head, 0)
        squares = lax.fori_loop(lag, chunks + lag, body, zero)

    size = two_site.shape[0] * two_site.shape[1] * two_site.shape[2]
    scale = lax.rsqrt(jnp.full((1, 1), jnp.sum(squares), F32) / size + epsilon)

    lanes = out_ref.shape[1]
    halves = two_site.shape[2] // lanes
    stride = PHYS * PHYS * halves
    for s in range(PHYS):
        for t in range(PHYS):
            for c in range(halves):
                span = pl.ds((s * halves + c) * PHYS + t, two_site.shape[1], stride=stride)
                columns = pl.ds(c * lanes, lanes)
                out_ref[span, :] = two_site[PHYS * s + t, :, columns] * scale

    iso_copy.wait_send()
    last_copy.wait_send()

    def drain_term(k, carry):
        env_copy(k).wait_send()

        @pl.when(is_odd)
        def _():
            fresh_copy(k).wait_send()

        return carry

    lax.fori_loop(0, terms, drain_term, 0)
    for n in range(STEPS):

        def drain_chunk(x, carry):
            in_copy(n, x).wait_send()

            @pl.when(has_outward)
            def _():
                out_copy(n, x).wait_send()

            return carry

        lax.fori_loop(0, chunks, drain_chunk, 0)


def shards(n_sec, n_term, meet_env, meet_iso, last_site, first_site, term_kind):
    terms, bond = meet_env.shape[1], meet_env.shape[2]
    pairs = PHYS * PHYS

    def by_level(site):
        return jnp.transpose(site[0], (1, 0, 2))

    vmem = pl.BlockSpec(memory_space=pltpu.VMEM)
    block = (bond, bond)
    chunks = pairs * PARTS
    strip = (bond // PARTS, bond)
    lanes = min(bond, 128)
    dma = pltpu.SemaphoreType.DMA
    out = pl.pallas_call(
        functools.partial(kernel, n_sec, n_term, terms),
        out_shape=jax.ShapeDtypeStruct((pairs * bond * bond // lanes, lanes), F32),
        in_specs=[pl.BlockSpec(memory_space=pltpu.SMEM)] + [vmem] * 4,
        out_specs=vmem,
        scratch_shapes=[
            pltpu.VMEM((2, terms) + block, BF16),
            pltpu.VMEM((terms,) + block, BF16),
            pltpu.VMEM((terms,) + block, BF16),
            pltpu.VMEM((PHYS,) + block, BF16),
            pltpu.VMEM((PHYS,) + block, BF16),
            pltpu.VMEM((2, PHYS) + block, BF16),
            pltpu.VMEM((2, 3) + block, BF16),
            pltpu.VMEM((STEPS, terms, pairs) + block, BF16),
            pltpu.VMEM((pairs,) + block, BF16),
            pltpu.VMEM((pairs,) + block, F32),
            pltpu.VMEM((pairs,) + block, F32),
            pltpu.VMEM((STEPS, chunks) + strip, BF16),
            pltpu.VMEM((STEPS, chunks) + strip, BF16),
            pltpu.VMEM((STEPS, 2, chunks) + strip, BF16),
            dma((2,)),
            dma((2,)),
            dma((terms,)),
            dma((terms,)),
            dma((terms,)),
            dma((terms,)),
            dma((STEPS, chunks)),
            dma((STEPS, 2, chunks)),
            dma((STEPS, chunks)),
        ],
        compiler_params=pltpu.CompilerParams(
            collective_id=0, has_side_effects=True, vmem_limit_bytes=48 * 1024 * 1024
        ),
    )(term_kind, meet_env[0], by_level(meet_iso), by_level(last_site), by_level(first_site))
    out = out.reshape(bond, PHYS, bond // lanes, PHYS, lanes)
    out = jnp.transpose(out, (0, 1, 3, 2, 4))
    return out.reshape(1, bond, PHYS, PHYS, bond)


def solution(mesh):
    in_specs = (
        P("sec", "term", None, None),
        P("sec", None, None, None),
        P("sec", None, None, None),
        P("sec", None, None, None),
        P("term", None),
    )
    out_specs = P("sec", None, None, None, None)
    body = functools.partial(shards, mesh.shape["sec"], mesh.shape["term"])
    return jax.shard_map(body, mesh=mesh, in_specs=in_specs, out_specs=out_specs, check_vma=False)
```
